32 devices in a mesh: cuts: 4 (over y, core), mesh: 8 (over z, x).
Axes of the slice: x: 2, y: 2, z: 4, core: 2. Of those that a mesh axis runs over, the one named last changes fastest.
Arguments:
- start_modes: float32 [128, 16384], P('cuts', 'mesh'), may hold values from -6 to 6
- connectivity: int32 [125, 256], P(None, 'mesh'), may hold values from 0 to 2047, as said below
- stiffness_weights: float32 [125, 256], P(None, 'mesh'), may hold values from 0.5 to 4
- shared_nodes: int32 [2, 4096], P(None, 'mesh'), may hold values from 0 to 2047, as said below
- node_mass: float32 [16384], P('mesh'), may hold values from 0.5 to 54
- centers: float32 [4], P('cuts'), may hold values from 20 to 200
- half_widths: float32 [4], P('cuts'), may hold values from 100 to 400
- keep_flags: int32 [4, 8], P('cuts'), may hold values 0 or 1
Outputs:
- filtered: float32 [128, 16384], P('cuts', 'mesh')
- edge_products: float32 [4, 8, 8], P('cuts')
- first_level: float32 [128, 16384], P('cuts', 'mesh')
The draws below stay inside these ranges and needn't reach their ends.
Inputs may be any that keep to these rules, and one draw needn't show every extreme that they name: `connectivity`: within each partition: entry k = 25 a + 5 b + c names the element's GLL node (a, b, c); every node index of the partition is named by some element, and neighbouring elements name the same nodes on their common faces. `shared_nodes`: within each partition the 1024 entries are distinct; entry k of row 1 of partition p and entry k of row 0 of partition p + 1 are copies of the same node.
All inputs are finite; a program needn't handle non-finite values. No bound on the sum of `keep_flags` on one device may be relied on, other than what follows from the above.
Results may differ from the reference program's by a relative error of at most 0.0001.
Values sent between devices are 32-bit elements; how exact they have to be, the bound alone decides.
A program may use at most 64 MiB of HBM per device.

```python
import math
import jax
import jax.numpy as jnp
import numpy as np
from jax import lax

MODES = 32
EDGE = 8
ELEM_DEV = 32
SHARED = 512
NODES_DEV = 2048
ELEMS = 256
NODES = 16384
N_CUTS = 4
N_MESH = 8


def node_labels(key):
    partitions = NODES // NODES_DEV

    def one_part(part_index):
        inner = jax.random.permutation(jax.random.fold_in(jax.random.fold_in(key, 71), part_index), NODES_DEV - 2) + 1
        return jnp.concatenate([jnp.zeros((1,), jnp.int32), inner.astype(jnp.int32), jnp.full((1,), NODES_DEV - 1, jnp.int32)])
    return jax.vmap(one_part)(jnp.arange(partitions))


def draw_connectivity(key, part):
    labels = node_labels(key)
    partitions = NODES // NODES_DEV
    span_x = NODES_DEV // 512
    element = jnp.arange(ELEM_DEV)
    elem_z = element % 8
    elem_y = element // 8 % 4
    elem_x = element // 32
    entry = jnp.arange(125)
    node_a = entry // 25
    node_b = entry // 5 % 5
    node_c = entry % 5
    pos_x = (4 * elem_x[None, :] + node_a[:, None]) % span_x
    pos_y = (4 * elem_y[None, :] + node_b[:, None]) % 16
    pos_z = (4 * elem_z[None, :] + node_c[:, None]) % 32
    lattice = (pos_x * 16 + pos_y) * 32 + pos_z
    per_part = jnp.take(labels, lattice, axis=1)

    def shuffle(part_index, columns):
        column_order = jax.random.permutation(jax.random.fold_in(jax.random.fold_in(key, 83), part_index), ELEM_DEV)
        return jnp.take(columns, column_order.astype(jnp.int32), axis=1)
    per_part = jax.vmap(shuffle)(jnp.arange(partitions), per_part)
    return per_part.transpose(1, 0, 2).reshape(125, ELEM_DEV * partitions).astype(jnp.int32)


def draw_shared_nodes(key, part):
    labels = node_labels(key)
    partitions = NODES // NODES_DEV

    def pairing(part_index):
        return jax.random.permutation(jax.random.fold_in(jax.random.fold_in(key, 89), part_index), SHARED).astype(jnp.int32)
    pairings = jax.vmap(pairing)(jnp.arange(partitions))
    shifted_pairs = jnp.roll(pairings, 1, axis=0)
    lower = jnp.take_along_axis(labels[:, :SHARED], shifted_pairs, axis=1)
    upper = jnp.take_along_axis(labels[:, NODES_DEV - SHARED:], pairings, axis=1)
    return jnp.stack([lower, upper]).reshape(2, partitions * SHARED).astype(jnp.int32)


def draw_node_mass(key, part):
    partitions = NODES // NODES_DEV
    rising = (jnp.arange(NODES) // NODES_DEV).astype(jnp.float32) / (partitions - 1)
    base = jnp.exp(jax.random.uniform(key, (NODES,), jnp.float32, math.log(0.5), math.log(5.0)))
    return base * 3.0 ** rising


def with_ends(drawn, rng, smallest, largest):
    dims = drawn.shape
    index_at = [jax.random.randint(jax.random.fold_in(rng, axis), (), 0, dims[axis]) for axis in range(len(dims))]
    drawn = drawn.at[tuple(index_at)].set(smallest)
    longest = dims.index(max(dims))
    index_at[longest] = (index_at[longest] + 1) % dims[longest]
    return drawn.at[tuple(index_at)].set(largest)


def steps_of(rng, dims, cuts, low, high):
    factor_of = 1.0
    for dim, blocks in cuts:
        steps = jax.random.uniform(jax.random.fold_in(jax.random.fold_in(rng, 6), dim), (blocks,), jnp.float32, low / len(cuts), high / len(cuts))
        factor_of = factor_of * jnp.repeat(jnp.exp(steps), dims[dim] // blocks).reshape((-1,) + (1,) * (len(dims) - 1 - dim))
    return factor_of


def centred(stream_key, shape, spread, most, cuts=(), kind=jnp.bfloat16):
    loudness = steps_of(stream_key, shape, cuts, -0.22, 0.18) if cuts else 1.0
    values = jax.random.normal(stream_key, shape, jnp.float32) * spread * loudness
    return jnp.minimum(jnp.maximum(values, -most), most).astype(kind)


def setup_inputs(seed: int = 0) -> dict:
    arg_keys = jax.random.split(jax.random.key(seed), 9)
    start_modes = centred(arg_keys[0], (N_CUTS * MODES, NODES), 1.0, 6.0, ((0, 4), (1, 8)), jnp.float32)
    connectivity = draw_connectivity(jax.random.fold_in(arg_keys[8], 71), 0)
    stiffness_weights = jnp.clip(jnp.exp(math.log(4.0) - 2.0794415 * jax.random.uniform(arg_keys[2], (125, ELEMS), jnp.float32) ** steps_of(arg_keys[2], (125, ELEMS), ((1, 8),), -0.2, 0.2)), 0.5, 4.0)
    shared_nodes = draw_shared_nodes(jax.random.fold_in(arg_keys[8], 71), 0)
    node_mass = draw_node_mass(jax.random.fold_in(arg_keys[8], 71), 0)
    centers = jnp.clip(20.0 + 180.0 * jax.random.uniform(arg_keys[5], (N_CUTS,), jnp.float32) ** steps_of(arg_keys[5], (N_CUTS,), ((0, 4),), -0.2, 0.2), 20.0, 200.0)
    half_widths = jnp.clip(jnp.exp(math.log(400.0) - 1.3862944 * jax.random.uniform(arg_keys[6], (N_CUTS,), jnp.float32) ** steps_of(arg_keys[6], (N_CUTS,), ((0, 4),), -0.2, 0.2)), 100.0, 400.0)
    keep_flags = with_ends((jax.random.randint(arg_keys[7], (N_CUTS, EDGE), 0, 4) < 3).astype(jnp.int32), jax.random.fold_in(arg_keys[7], 1), 0, 1)
    return {"start_modes": start_modes, "connectivity": connectivity, "stiffness_weights": stiffness_weights, "shared_nodes": shared_nodes, "node_mass": node_mass, "centers": centers, "half_widths": half_widths, "keep_flags": keep_flags}


epsilon = 1e-06
highest = lax.Precision.HIGHEST

def gll_derivative():
    points = np.array([-1.0, -math.sqrt(3.0 / 7.0), 0.0, math.sqrt(3.0 / 7.0), 1.0])
    barycentric = np.array([1.0 / np.prod([points[j] - points[k] for k in range(5) if k != j]) for j in range(5)])
    table = np.zeros((5, 5))
    for row_index in range(5):
        for col_index in range(5):
            if row_index != col_index:
                table[row_index, col_index] = barycentric[col_index] / barycentric[row_index] / (points[row_index] - points[col_index])
        table[row_index, row_index] = -np.sum(table[row_index])
    return table

def stiffness(fields, conn_part, weight_part, derivative):
    row_count = fields.shape[0]
    elements = conn_part.shape[1]
    values = jnp.take(fields, conn_part, axis=1).reshape(row_count, 5, 5, 5, elements)
    weight = weight_part.reshape(5, 5, 5, elements)
    grad_a = jnp.einsum('ia,mabce->mibce', derivative, values, precision=highest)
    grad_b = jnp.einsum('jb,mabce->majce', derivative, values, precision=highest)
    grad_c = jnp.einsum('kc,mabce->mabke', derivative, values, precision=highest)
    returned = jnp.einsum('ia,mibce->mabce', derivative, weight * grad_a, precision=highest)
    returned = returned + jnp.einsum('jb,majce->mabce', derivative, weight * grad_b, precision=highest)
    returned = returned + jnp.einsum('kc,mabke->mabce', derivative, weight * grad_c, precision=highest)
    returned = returned.reshape(row_count, 125, elements)
    return jnp.zeros(fields.shape, fields.dtype).at[:, conn_part].add(returned)

def operate(fields, connectivity, stiffness_weights, shared_nodes, node_mass, derivative):
    row_count = fields.shape[0]
    per_part = fields.reshape(row_count, N_MESH, NODES_DEV).transpose(1, 0, 2)
    conn_parts = connectivity.reshape(125, N_MESH, ELEM_DEV).transpose(1, 0, 2)
    weight_parts = stiffness_weights.reshape(125, N_MESH, ELEM_DEV).transpose(1, 0, 2)
    applied = lax.map(lambda bundle: stiffness(bundle[0], bundle[1], bundle[2], derivative), (per_part, conn_parts, weight_parts))
    shared_parts = shared_nodes.reshape(2, N_MESH, SHARED).transpose(1, 0, 2)
    lower_vals = jax.vmap(lambda values_part, index_part: values_part[:, index_part])(applied, shared_parts[:, 0])
    upper_vals = jax.vmap(lambda values_part, index_part: values_part[:, index_part])(applied, shared_parts[:, 1])
    padding = jnp.zeros((1, row_count, SHARED), applied.dtype)
    from_below = jnp.concatenate([padding, upper_vals[:-1]], axis=0)
    from_above = jnp.concatenate([lower_vals[1:], padding], axis=0)
    adder = jax.vmap(lambda values_part, index_part, extra: values_part.at[:, index_part].add(extra))
    applied = adder(applied, shared_parts[:, 0], from_below)
    applied = adder(applied, shared_parts[:, 1], from_above)
    return applied.transpose(1, 0, 2).reshape(row_count, NODES) / node_mass

def reference(start_modes, connectivity, stiffness_weights, shared_nodes, node_mass, centers, half_widths, keep_flags):
    derivative = jnp.asarray(gll_derivative(), jnp.float32)
    filtered_list = []
    level_list = []
    for cut_index in range(N_CUTS):
        start = start_modes[cut_index * MODES:(cut_index + 1) * MODES]
        center = centers[cut_index]
        half_width = half_widths[cut_index]
        first_step = (operate(start, connectivity, stiffness_weights, shared_nodes, node_mass, derivative) - center * start) / half_width
        first_norms = lax.optimization_barrier(jnp.sum(node_mass * first_step * first_step, axis=1))
        first_scale = lax.rsqrt(first_norms / NODES + epsilon)
        level_one = first_step * first_scale[:, None]
        level_zero = start * first_scale[:, None]
        applied = operate(level_one, connectivity, stiffness_weights, shared_nodes, node_mass, derivative)
        second_step = 2.0 * (applied - center * level_one) / half_width - level_zero
        second_norms = lax.optimization_barrier(jnp.sum(node_mass * second_step * second_step, axis=1))
        filtered_list.append(second_step * lax.rsqrt(second_norms / NODES + epsilon)[:, None])
        level_list.append(level_one)
    products = [jnp.zeros((EDGE, EDGE), jnp.float32)]
    for cut_index in range(1, N_CUTS):
        upper_rows = filtered_list[cut_index - 1][MODES - EDGE:] * node_mass
        lower_rows = filtered_list[cut_index][:EDGE]
        inner = jnp.einsum('in,jn->ij', upper_rows, lower_rows, precision=highest)
        products.append(inner * keep_flags[cut_index].astype(jnp.float32)[None, :] / math.sqrt(NODES))
    return (jnp.concatenate(filtered_list, axis=0), jnp.stack(products), jnp.concatenate(level_list, axis=0))
```

```python
import functools
import math

import jax
import jax.numpy as jnp
import numpy as np
from jax import lax
from jax.experimental import pallas as pl
from jax.experimental.pallas import tpu as pltpu
from jax.sharding import PartitionSpec as P

epsilon = 1e-06
TILE = 256
MESH = pl.DeviceIdType.MESH
bf16 = jnp.bfloat16
f32 = jnp.float32


def gll_derivative():
    points = np.array([-1.0, -math.sqrt(3.0 / 7.0), 0.0, math.sqrt(3.0 / 7.0), 1.0])
    barycentric = np.array(
        [1.0 / np.prod([points[j] - points[k] for k in range(5) if k != j]) for j in range(5)]
    )
    table = np.zeros((5, 5))
    for row_index in range(5):
        for col_index in range(5):
            if row_index != col_index:
                table[row_index, col_index] = (
                    barycentric[col_index]
                    / barycentric[row_index]
                    / (points[row_index] - points[col_index])
                )
        table[row_index, row_index] = -np.sum(table[row_index])
    return table


def apply5(table, u):
    even = [u[0] + u[4], u[1] + u[3]]
    odd = [u[0] - u[4], u[1] - u[3]]
    out = [None] * 5
    for i in range(2):
        s = [float((table[i, j] + table[i, 4 - j]) / 2) for j in range(2)]
        t = [float((table[i, j] - table[i, 4 - j]) / 2) for j in range(2)]
        p = s[0] * even[0] + s[1] * even[1] + float(table[i, 2]) * u[2]
        q = t[0] * odd[0] + t[1] * odd[1]
        out[i] = q + p
        out[4 - i] = q - p
    t = [float((table[2, j] - table[2, 4 - j]) / 2) for j in range(2)]
    out[2] = t[0] * odd[0] + t[1] * odd[1]
    return out


def transpose4(x):
    block = lax.broadcasted_iota(jnp.int32, x[0].shape, 1) // 32
    at = [block == b for b in range(3)]
    y = [x[0]] + [pltpu.roll(x[g], 32 * g, 1) for g in range(1, 4)]
    z = []
    for q in range(4):
        w = y[(3 - q) % 4]
        for b in range(3):
            w = jnp.where(at[b], y[(b - q) % 4], w)
        z.append(w if q == 0 else pltpu.roll(w, 128 - 32 * q, 1))
    return z


def split2(x):
    high = x.astype(bf16)
    low = (x - high.astype(f32)).astype(bf16)
    return high, low


def kernel(
    n_mesh,
    n_cuts,
    total_nodes,
    v_ref,
    conn_ref,
    w_ref,
    shared_ref,
    mass_ref,
    center_ref,
    half_ref,
    first_s,
    second_s,
    total_ref,
    turn_s,
    conn_s,
    low_s,
    high_s,
    sh_low,
    sh_high,
    w_s,
    u_s,
    r_s,
    tx,
    rx,
    edge_tx,
    edge_rx,
    block,
    blocks,
    halo_send,
    halo_recv,
    edge_send,
    edge_recv,
    sum_send,
    sum_recv,
):
    me = lax.axis_index("mesh")
    cut = lax.axis_index("cuts")
    modes, nodes = v_ref.shape
    groups = modes // 8
    low_size = 2 * TILE if nodes % (2 * TILE) == 0 else TILE
    highs = nodes // low_size
    shift = low_size.bit_length() - 1
    elements, local = conn_ref.shape
    shared = shared_ref.shape[1]
    edge_count = edge_tx.shape[0]
    table = gll_derivative()

    barrier = pltpu.get_barrier_semaphore()

    def greet(d, carry):
        pl.semaphore_signal(
            barrier,
            inc=1,
            device_id={"mesh": lax.rem(me + d, n_mesh)},
            device_id_type=MESH,
        )
        return carry

    lax.fori_loop(1, n_mesh, greet, 0)

    @pl.when(cut > 0)
    def _():
        pl.semaphore_signal(
            barrier, inc=1, device_id={"cuts": cut - 1}, device_id_type=MESH
        )

    @pl.when(cut < n_cuts - 1)
    def _():
        pl.semaphore_signal(
            barrier, inc=1, device_id={"cuts": cut + 1}, device_id_type=MESH
        )

    turn_s[...] = jnp.full(turn_s.shape, -1.0, f32)
    turn_s[0:elements, 0:local] = conn_ref[...].astype(f32)
    turn_s[elements : 2 * elements, 0:local] = w_ref[...]
    turned = turn_s[...].T
    conn_s[...] = turned[:, 0:elements].astype(jnp.int32)
    chunks = conn_s.shape[0] // 4
    index = jnp.concatenate(
        [conn_s[pl.ds(q, chunks, stride=4), :] for q in range(4)], axis=1
    )
    iota = lax.broadcasted_iota(jnp.int32, (16, 128), 0)
    steps = [(iota + 16 * i).astype(f32).astype(bf16) for i in range(TILE // 16)]
    one = jnp.ones((16, 128), bf16)
    zero = jnp.zeros((16, 128), bf16)

    def onehot(low_ref, r):
        row = low_ref[r : r + 1, :]
        parts = []
        for t in range(low_size // TILE):
            wide = jnp.broadcast_to(row - float(TILE * t), (16, 128)).astype(bf16)
            parts += [jnp.where(step == wide, one, zero) for step in steps]
        return jnp.concatenate(parts, axis=0)

    low_s[...] = (index & (low_size - 1)).astype(f32)
    high_s[...] = (index >> shift).astype(f32)
    per_row = shared // 128
    for r in range(2 * per_row):
        side, at = r // per_row, r % per_row * 128
        row = shared_ref[side : side + 1, at : at + 128]
        sh_low[r : r + 1, :] = (row & (low_size - 1)).astype(f32)
        sh_high[r : r + 1, :] = (row >> shift).astype(f32)
    w4 = jnp.concatenate([turned[:, elements : 2 * elements]] * 4, axis=1)
    for k in range(local):
        w_s[k] = jnp.broadcast_to(w4[k : k + 1], (8, 128))
    r_s[local:] = jnp.zeros((r_s.shape[0] - local, 8, 128), f32)

    inv_mass = 1.0 / mass_ref[...]
    center = center_ref[0]
    inv_half = 1.0 / jnp.full((1, 128), half_ref[0], f32)[:, 0:1]

    rows = highs * modes

    def load_source(x):
        parts = split2(x)
        return jnp.concatenate(
            [y[:, h * low_size : (h + 1) * low_size] for y in parts for h in range(highs)], axis=0
        )

    def gather(left, low_ref, high_ref, t):
        right = jnp.concatenate([onehot(low_ref, 2 * t), onehot(low_ref, 2 * t + 1)], axis=1)
        res = jnp.dot(left, right, preferred_element_type=f32)
        res = res[0:rows] + res[rows:]
        out = []
        for half in range(2):
            at = 2 * t + half
            high = jnp.broadcast_to(high_ref[at : at + 1, :], (8, 128))
            cols = slice(half * 128, half * 128 + 128)
            sides = [high == h for h in range(1, highs)]
            groups_out = []
            for g in range(groups):
                pick = res[g * 8 : g * 8 + 8, cols]
                for h in range(1, highs):
                    at = h * modes + g * 8
                    pick = jnp.where(sides[h - 1], res[at : at + 8, cols], pick)
                groups_out.append(pick)
            out.append(groups_out)
        return out

    def place(x, high_ref, r):
        high = jnp.broadcast_to(high_ref[r : r + 1, :], (16, 128)).astype(bf16)
        parts = split2(x)
        out = []
        for h in range(highs):
            here = high == jnp.full((16, 128), h, bf16)
            for y in parts:
                for i in range(modes // 16):
                    out.append(jnp.where(here, y[i * 16 : i * 16 + 16], zero))
        return jnp.concatenate(out, axis=0)

    def scatter(placed, low_ref):
        res = lax.dot_general(
            jnp.concatenate(placed, axis=1),
            jnp.concatenate([onehot(low_ref, r) for r in range(len(placed))], axis=1),
            (((1,), (1,)), ((), ())),
            preferred_element_type=f32,
        )
        return jnp.concatenate(
            [
                res[h * 2 * modes : h * 2 * modes + modes]
                + res[h * 2 * modes + modes : (h + 1) * 2 * modes]
                for h in range(highs)
            ],
            axis=1,
        )

    def line(u, w):
        g = apply5(table, u)
        return apply5(table.T, [g[i] * w[i] for i in range(5)])

    def element_pass():
        for a in range(5):
            u = [u_s[25 * a + j] for j in range(25)]
            w = [w_s[25 * a + j] for j in range(25)]
            r = [None] * 25
            for b in range(5):
                r[5 * b : 5 * b + 5] = line(u[5 * b : 5 * b + 5], w[5 * b : 5 * b + 5])
            for c in range(5):
                back = line(u[c::5], w[c::5])
                for b in range(5):
                    r_s[25 * a + 5 * b + c] = r[5 * b + c] + back[b]
        for j in range(25):
            back = line([u_s[25 * a + j] for a in range(5)], [w_s[25 * a + j] for a in range(5)])
            for a in range(5):
                r_s[25 * a + j] = r_s[25 * a + j] + back[a]

    def halo(step):
        up = pltpu.make_async_remote_copy(
            src_ref=tx.at[step, 1],
            dst_ref=rx.at[step, 0],
            send_sem=halo_send.at[step, 0],
            recv_sem=halo_recv.at[step, 0],
            device_id={"mesh": lax.rem(me + 1, n_mesh)},
            device_id_type=MESH,
        )
        down = pltpu.make_async_remote_copy(
            src_ref=tx.at[step, 0],
            dst_ref=rx.at[step, 1],
            send_sem=halo_send.at[step, 1],
            recv_sem=halo_recv.at[step, 1],
            device_id={"mesh": lax.rem(me + n_mesh - 1, n_mesh)},
            device_id_type=MESH,
        )
        return up, down

    @pl.when(me == 0)
    def _():
        for step in range(2):
            rx[step, 0] = jnp.zeros((modes, shared), f32)

    @pl.when(me == n_mesh - 1)
    def _():
        for step in range(2):
            rx[step, 1] = jnp.zeros((modes, shared), f32)

    @pl.when(cut == 0)
    def _():
        edge_rx[...] = jnp.zeros(edge_rx.shape, f32)

    def operate(x, step, between):
        left = load_source(x)
        for t in range(chunks // 2):
            out = gather(left, low_s, high_s, t)
            for half in range(2):
                r = 2 * t + half
                for q, y in enumerate(transpose4(out[half])):
                    u_s[4 * r + q] = y
        element_pass()
        placed = []
        for r in range(chunks):
            piece = transpose4([r_s[4 * r + q] for q in range(4)])
            placed.append(place(jnp.concatenate(piece, axis=0), high_s, r))
        applied = scatter(placed, low_s)
        left = load_source(applied)
        up, down = halo(step)
        for t in range(2 * shared // 256):
            out = gather(left, sh_low, sh_high, t)
            at = t * 256
            tx[step, at // shared, :, at % shared : at % shared + 256] = jnp.concatenate(
                [jnp.concatenate(half, axis=0) for half in out], axis=1
            )
            if at + 256 == shared:
                if step == 0:
                    pl.semaphore_wait(
                        barrier,
                        n_mesh - 1 + jnp.minimum(cut, 1) + jnp.minimum(n_cuts - 1 - cut, 1),
                    )

                @pl.when(me > 0)
                def _():
                    down.start()

        @pl.when(me < n_mesh - 1)
        def _():
            up.start()

        between()

        @pl.when(me > 0)
        def _():
            up.wait_recv()

        @pl.when(me < n_mesh - 1)
        def _():
            down.wait_recv()

        placed = []
        for side in range(2):
            for j in range(per_row):
                x_in = rx[step, side, :, j * 128 : j * 128 + 128]
                placed.append(place(x_in, sh_high, side * per_row + j))
        return (applied + scatter(placed, sh_low)) * inv_mass

    start = v_ref[...]
    mass = mass_ref[...]
    turn_s[...] = jnp.zeros(turn_s.shape, f32)

    def masks():
        pass

    def first_column():
        level = first_s[...]
        lane = lax.broadcasted_iota(jnp.int32, (modes, 128), 1)
        turn_s[0:modes, :] = jnp.where(
            lane == 0, jnp.sum(mass * level * level, axis=1, keepdims=True), 0.0
        )

    first_s[...] = (operate(start, 0, masks) - center * start) * inv_half
    first = first_s[...]
    second_s[...] = 2.0 * (operate(first, 1, first_column) - center * first_s[...]) * inv_half - v_ref[...]

    first_sum = turn_s[0:modes, 0:1]
    edge_tx[:, 0:nodes] = second_s[modes - edge_count :, :]
    edge_tx[:, nodes:] = jnp.broadcast_to(first_sum[modes - edge_count :], (edge_count, 128))
    edge_copy = pltpu.make_async_remote_copy(
        src_ref=edge_tx,
        dst_ref=edge_rx,
        send_sem=edge_send,
        recv_sem=edge_recv,
        device_id={"cuts": lax.rem(cut + 1, n_cuts)},
        device_id_type=MESH,
    )

    @pl.when(cut < n_cuts - 1)
    def _():
        edge_copy.start()

    second = second_s[...]
    second_sum = jnp.sum(mass * second * second, axis=1, keepdims=True)

    def columns(a, b):
        lane = lax.broadcasted_iota(jnp.int32, (a.shape[0], 128), 1)
        return jnp.where(lane == 0, a, jnp.where(lane == 1, b, 0.0))

    turn_s[0:modes, :] = columns(first_sum, second_sum)

    @pl.when(cut > 0)
    def _():
        edge_copy.wait_recv()

    received = edge_rx[:, 0:nodes]
    weighted = received * mass
    turn_s[modes : modes + edge_count, :] = columns(
        edge_rx[:, nodes:][:, 0:1], jnp.sum(weighted * received, axis=1, keepdims=True)
    )
    inner = lax.dot_general(
        weighted,
        second,
        (((1,), (1,)), ((), ())),
        preferred_element_type=f32,
        precision=lax.Precision.HIGHEST,
    )
    turn_s[modes + edge_count : modes + 2 * edge_count, 0:modes] = inner
    block[...] = turn_s[...].T[0:8]

    def sum_copy(d):
        return pltpu.make_async_remote_copy(
            src_ref=block,
            dst_ref=blocks.at[me],
            send_sem=sum_send.at[d],
            recv_sem=sum_recv.at[d],
            device_id={"mesh": lax.rem(me + d, n_mesh)},
            device_id_type=MESH,
        )

    def start_sum(d, carry):
        sum_copy(d).start()
        return carry

    lax.fori_loop(1, n_mesh, start_sum, 0)
    blocks[me] = block[...]

    def wait_sum(d, carry):
        sum_copy(d).wait_recv()
        return carry

    lax.fori_loop(1, n_mesh, wait_sum, 0)
    total = lax.fori_loop(1, n_mesh, lambda i, acc: acc + blocks[i], blocks[0])

    total_ref[...] = total

    for step in range(2):
        up, down = halo(step)

        @pl.when(me < n_mesh - 1)
        def _():
            up.wait_send()

        @pl.when(me > 0)
        def _():
            down.wait_send()

    @pl.when(cut < n_cuts - 1)
    def _():
        edge_copy.wait_send()

    def wait_sent(d, carry):
        sum_copy(d).wait_send()
        return carry

    lax.fori_loop(1, n_mesh, wait_sent, 0)


def finish(total_nodes, first_ref, second_ref, total_ref, keep_ref, filt_ref, edge_ref, level_ref):
    modes = first_ref.shape[0]
    edge_count = keep_ref.shape[1]
    total = jnp.concatenate([total_ref[...], jnp.zeros((120, 128), f32)], axis=0).T
    scale = lax.rsqrt(total[:, 0:1] / total_nodes + epsilon)
    own = scale * lax.rsqrt(scale * scale * total[:, 1:2] / total_nodes + epsilon)
    level_ref[...] = first_ref[...] * scale[0:modes]
    filt_ref[...] = second_ref[...] * own[0:modes]
    eye = lax.broadcasted_iota(jnp.int32, (modes, modes), 0) == lax.broadcasted_iota(
        jnp.int32, (modes, modes), 1
    )
    own_row = jnp.sum(
        jnp.where(eye, jnp.broadcast_to(own[0:modes], (modes, modes)), 0.0),
        axis=0,
        keepdims=True,
    )
    products = (
        total[modes + edge_count : modes + 2 * edge_count, 0:edge_count]
        * own[modes : modes + edge_count]
        * own_row[:, 0:edge_count]
        * keep_ref[...].astype(f32)
        * (1.0 / math.sqrt(total_nodes))
    )
    edge_ref[0] = products


def per_device(
    start_modes,
    connectivity,
    stiffness_weights,
    shared_nodes,
    node_mass,
    centers,
    half_widths,
    keep_flags,
):
    n_mesh = lax.axis_size("mesh")
    n_cuts = lax.axis_size("cuts")
    modes, nodes = start_modes.shape
    local, elements = connectivity.shape
    shared = shared_nodes.shape[1]
    edge_count = keep_flags.shape[1]
    padded = -(-local // 8) * 8
    chunks = padded * elements // 128
    pairs = 2 * shared // 128
    vmem = pl.BlockSpec(memory_space=pltpu.VMEM)
    smem = pl.BlockSpec(memory_space=pltpu.SMEM)
    dma = pltpu.SemaphoreType.DMA
    first, second, total = pl.pallas_call(
        functools.partial(kernel, n_mesh, n_cuts, nodes * n_mesh),
        out_shape=(
            jax.ShapeDtypeStruct((modes, nodes), f32),
            jax.ShapeDtypeStruct((modes, nodes), f32),
            jax.ShapeDtypeStruct((8, 128), f32),
        ),
        in_specs=[vmem, vmem, vmem, vmem, vmem, smem, smem],
        out_specs=(vmem, vmem, vmem),
        scratch_shapes=[
            pltpu.VMEM((128, 128), f32),
            pltpu.VMEM((padded, elements), jnp.int32),
            pltpu.VMEM((chunks, 128), f32),
            pltpu.VMEM((chunks, 128), f32),
            pltpu.VMEM((pairs, 128), f32),
            pltpu.VMEM((pairs, 128), f32),
            pltpu.VMEM((padded, 8, 128), f32),
            pltpu.VMEM((padded, 8, 128), f32),
            pltpu.VMEM((padded, 8, 128), f32),
            pltpu.VMEM((2, 2, modes, shared), f32),
            pltpu.VMEM((2, 2, modes, shared), f32),
            pltpu.VMEM((edge_count, nodes + 128), f32),
            pltpu.VMEM((edge_count, nodes + 128), f32),
            pltpu.VMEM((8, 128), f32),
            pltpu.VMEM((n_mesh, 8, 128), f32),
            dma((2, 2)),
            dma((2, 2)),
            dma,
            dma,
            dma((n_mesh,)),
            dma((n_mesh,)),
        ],
        compiler_params=pltpu.CompilerParams(collective_id=0, has_side_effects=True),
    )(
        start_modes,
        connectivity.T,
        stiffness_weights.T,
        shared_nodes,
        node_mass.reshape(1, nodes),
        centers,
        half_widths,
    )
    return pl.pallas_call(
        functools.partial(finish, nodes * n_mesh),
        out_shape=(
            jax.ShapeDtypeStruct((modes, nodes), f32),
            jax.ShapeDtypeStruct((1, edge_count, edge_count), f32),
            jax.ShapeDtypeStruct((modes, nodes), f32),
        ),
        in_specs=[vmem, vmem, vmem, vmem],
        out_specs=(vmem, vmem, vmem),
    )(first, second, total, keep_flags)


def solution(mesh):
    return jax.shard_map(
        per_device,
        mesh=mesh,
        in_specs=(
            P("cuts", "mesh"),
            P(None, "mesh"),
            P(None, "mesh"),
            P(None, "mesh"),
            P("mesh"),
            P("cuts"),
            P("cuts"),
            P("cuts", None),
        ),
        out_specs=(P("cuts", "mesh"), P("cuts", None, None), P("cuts", "mesh")),
        check_vma=False,
    )
```

```python
import functools
import math

import jax
import jax.numpy as jnp
import numpy as np
from jax import lax
from jax.experimental import pallas as pl
from jax.experimental.pallas import tpu as pltpu
from jax.sharding import PartitionSpec as P

epsilon = 1e-06
TILE = 256
MESH = pl.DeviceIdType.MESH
bf16 = jnp.bfloat16
f32 = jnp.float32


def gll_derivative():
    points = np.array([-1.0, -math.sqrt(3.0 / 7.0), 0.0, math.sqrt(3.0 / 7.0), 1.0])
    barycentric = np.array(
        [1.0 / np.prod([points[j] - points[k] for k in range(5) if k != j]) for j in range(5)]
    )
    table = np.zeros((5, 5))
    for row_index in range(5):
        for col_index in range(5):
            if row_index != col_index:
                table[row_index, col_index] = (
                    barycentric[col_index]
                    / barycentric[row_index]
                    / (points[row_index] - points[col_index])
                )
        table[row_index, row_index] = -np.sum(table[row_index])
    return table


def apply5(table, u):
    even = [u[0] + u[4], u[1] + u[3]]
    odd = [u[0] - u[4], u[1] - u[3]]
    out = [None] * 5
    for i in range(2):
        s = [float((table[i, j] + table[i, 4 - j]) / 2) for j in range(2)]
        t = [float((table[i, j] - table[i, 4 - j]) / 2) for j in range(2)]
        p = s[0] * even[0] + s[1] * even[1] + float(table[i, 2]) * u[2]
        q = t[0] * odd[0] + t[1] * odd[1]
        out[i] = q + p
        out[4 - i] = q - p
    t = [float((table[2, j] - table[2, 4 - j]) / 2) for j in range(2)]
    out[2] = t[0] * odd[0] + t[1] * odd[1]
    return out


def transpose4(x):
    block = lax.broadcasted_iota(jnp.int32, x[0].shape, 1) // 32
    at = [block == b for b in range(3)]
    y = [x[0]] + [pltpu.roll(x[g], 32 * g, 1) for g in range(1, 4)]
    z = []
    for q in range(4):
        w = y[(3 - q) % 4]
        for b in range(3):
            w = jnp.where(at[b], y[(b - q) % 4], w)
        z.append(w if q == 0 else pltpu.roll(w, 128 - 32 * q, 1))
    return z


def split2(x):
    high = x.astype(bf16)
    low = (x - high.astype(f32)).astype(bf16)
    return high, low


def kernel(
    n_mesh,
    n_cuts,
    total_nodes,
    v_ref,
    conn_ref,
    w_ref,
    shared_ref,
    mass_ref,
    center_ref,
    half_ref,
    first_s,
    second_s,
    total_ref,
    turn_s,
    conn_s,
    low_s,
    high_s,
    sh_low,
    sh_high,
    w_s,
    u_s,
    r_s,
    tx,
    rx,
    edge_tx,
    edge_rx,
    block,
    blocks,
    halo_send,
    halo_recv,
    edge_send,
    edge_recv,
    sum_send,
    sum_recv,
):
    me = lax.axis_index("mesh")
    cut = lax.axis_index("cuts")
    modes, nodes = v_ref.shape
    groups = modes // 8
    low_size = 2 * TILE if nodes % (2 * TILE) == 0 else TILE
    highs = nodes // low_size
    shift = low_size.bit_length() - 1
    elements, local = conn_ref.shape
    shared = shared_ref.shape[1]
    edge_count = edge_tx.shape[0]
    table = gll_derivative()

    barrier = pltpu.get_barrier_semaphore()

    def greet(d, carry):
        pl.semaphore_signal(
            barrier,
            inc=1,
            device_id={"mesh": lax.rem(me + d, n_mesh)},
            device_id_type=MESH,
        )
        return carry

    lax.fori_loop(1, n_mesh, greet, 0)

    @pl.when(cut > 0)
    def _():
        pl.semaphore_signal(
            barrier, inc=1, device_id={"cuts": cut - 1}, device_id_type=MESH
        )

    @pl.when(cut < n_cuts - 1)
    def _():
        pl.semaphore_signal(
            barrier, inc=1, device_id={"cuts": cut + 1}, device_id_type=MESH
        )

    turn_s[...] = jnp.full(turn_s.shape, -1.0, f32)
    turn_s[0:elements, 0:local] = conn_ref[...].astype(f32)
    turn_s[elements : 2 * elements, 0:local] = w_ref[...]
    turned = turn_s[...].T
    conn_s[...] = turned[:, 0:elements].astype(jnp.int32)
    chunks = conn_s.shape[0] // 4
    index = jnp.concatenate(
        [conn_s[pl.ds(q, chunks, stride=4), :] for q in range(4)], axis=1
    )
    iota = lax.broadcasted_iota(jnp.int32, (16, 128), 0)
    steps = [(iota + 16 * i).astype(f32).astype(bf16) for i in range(TILE // 16)]
    one = jnp.ones((16, 128), bf16)
    zero = jnp.zeros((16, 128), bf16)

    def onehot(low_ref, r):
        row = low_ref[r : r + 1, :]
        parts = []
        for t in range(low_size // TILE):
            wide = jnp.broadcast_to(row - float(TILE * t), (16, 128)).astype(bf16)
            parts += [jnp.where(step == wide, one, zero) for step in steps]
        return jnp.concatenate(parts, axis=0)

    low_s[...] = (index & (low_size - 1)).astype(f32)
    high_s[...] = (index >> shift).astype(f32)
    per_row = shared // 128
    for r in range(2 * per_row):
        side, at = r // per_row, r % per_row * 128
        row = shared_ref[side : side + 1, at : at + 128]
        sh_low[r : r + 1, :] = (row & (low_size - 1)).astype(f32)
        sh_high[r : r + 1, :] = (row >> shift).astype(f32)
    w4 = jnp.concatenate([turned[:, elements : 2 * elements]] * 4, axis=1)
    for k in range(local):
        w_s[k] = jnp.broadcast_to(w4[k : k + 1], (8, 128))
    r_s[local:] = jnp.zeros((r_s.shape[0] - local, 8, 128), f32)

    inv_mass = 1.0 / mass_ref[...]
    center = center_ref[...]
    inv_half = 1.0 / half_ref[...]

    rows = highs * modes

    def load_source(x):
        parts = split2(x)
        return jnp.concatenate(
            [y[:, h * low_size : (h + 1) * low_size] for y in parts for h in range(highs)], axis=0
        )

    def gather(left, low_ref, high_ref, t):
        right = jnp.concatenate([onehot(low_ref, 2 * t), onehot(low_ref, 2 * t + 1)], axis=1)
        res = jnp.dot(left, right, preferred_element_type=f32)
        res = res[0:rows] + res[rows:]
        out = []
        for half in range(2):
            at = 2 * t + half
            high = jnp.broadcast_to(high_ref[at : at + 1, :], (8, 128))
            cols = slice(half * 128, half * 128 + 128)
            sides = [high == h for h in range(1, highs)]
            groups_out = []
            for g in range(groups):
                pick = res[g * 8 : g * 8 + 8, cols]
                for h in range(1, highs):
                    at = h * modes + g * 8
                    pick = jnp.where(sides[h - 1], res[at : at + 8, cols], pick)
                groups_out.append(pick)
            out.append(groups_out)
        return out

    def place(x, high_ref, r):
        high = jnp.broadcast_to(high_ref[r : r + 1, :], (16, 128)).astype(bf16)
        parts = split2(x)
        out = []
        for h in range(highs):
            here = high == jnp.full((16, 128), h, bf16)
            for y in parts:
                for i in range(modes // 16):
                    out.append(jnp.where(here, y[i * 16 : i * 16 + 16], zero))
        return jnp.concatenate(out, axis=0)

    def scatter(placed, low_ref):
        res = lax.dot_general(
            jnp.concatenate(placed, axis=1),
            jnp.concatenate([onehot(low_ref, r) for r in range(len(placed))], axis=1),
            (((1,), (1,)), ((), ())),
            preferred_element_type=f32,
        )
        return jnp.concatenate(
            [
                res[h * 2 * modes : h * 2 * modes + modes]
                + res[h * 2 * modes + modes : (h + 1) * 2 * modes]
                for h in range(highs)
            ],
            axis=1,
        )

    def line(u, w):
        g = apply5(table, u)
        return apply5(table.T, [g[i] * w[i] for i in range(5)])

    def element_pass():
        for a in range(5):
            u = [u_s[25 * a + j] for j in range(25)]
            w = [w_s[25 * a + j] for j in range(25)]
            r = [None] * 25
            for b in range(5):
                r[5 * b : 5 * b + 5] = line(u[5 * b : 5 * b + 5], w[5 * b : 5 * b + 5])
            for c in range(5):
                back = line(u[c::5], w[c::5])
                for b in range(5):
                    r_s[25 * a + 5 * b + c] = r[5 * b + c] + back[b]
        for j in range(25):
            back = line([u_s[25 * a + j] for a in range(5)], [w_s[25 * a + j] for a in range(5)])
            for a in range(5):
                r_s[25 * a + j] = r_s[25 * a + j] + back[a]

    def halo(step):
        up = pltpu.make_async_remote_copy(
            src_ref=tx.at[step, 1],
            dst_ref=rx.at[step, 0],
            send_sem=halo_send.at[step, 0],
            recv_sem=halo_recv.at[step, 0],
            device_id={"mesh": lax.rem(me + 1, n_mesh)},
            device_id_type=MESH,
        )
        down = pltpu.make_async_remote_copy(
            src_ref=tx.at[step, 0],
            dst_ref=rx.at[step, 1],
            send_sem=halo_send.at[step, 1],
            recv_sem=halo_recv.at[step, 1],
            device_id={"mesh": lax.rem(me + n_mesh - 1, n_mesh)},
            device_id_type=MESH,
        )
        return up, down

    @pl.when(me == 0)
    def _():
        for step in range(2):
            rx[step, 0] = jnp.zeros((modes, shared), f32)

    @pl.when(me == n_mesh - 1)
    def _():
        for step in range(2):
            rx[step, 1] = jnp.zeros((modes, shared), f32)

    @pl.when(cut == 0)
    def _():
        edge_rx[...] = jnp.zeros(edge_rx.shape, f32)

    def operate(x, step, between):
        left = load_source(x)
        for t in range(chunks // 2):
            out = gather(left, low_s, high_s, t)
            for half in range(2):
                r = 2 * t + half
                for q, y in enumerate(transpose4(out[half])):
                    u_s[4 * r + q] = y
        element_pass()
        placed = []
        for r in range(chunks):
            piece = transpose4([r_s[4 * r + q] for q in range(4)])
            placed.append(place(jnp.concatenate(piece, axis=0), high_s, r))
        applied = scatter(placed, low_s)
        left = load_source(applied)
        up, down = halo(step)
        for t in range(2 * shared // 256):
            out = gather(left, sh_low, sh_high, t)
            at = t * 256
            tx[step, at // shared, :, at % shared : at % shared + 256] = jnp.concatenate(
                [jnp.concatenate(half, axis=0) for half in out], axis=1
            )
            if at + 256 == shared:
                if step == 0:
                    pl.semaphore_wait(
                        barrier,
                        n_mesh - 1 + jnp.minimum(cut, 1) + jnp.minimum(n_cuts - 1 - cut, 1),
                    )

                @pl.when(me > 0)
                def _():
                    down.start()

        @pl.when(me < n_mesh - 1)
        def _():
            up.start()

        between()

        @pl.when(me > 0)
        def _():
            up.wait_recv()

        @pl.when(me < n_mesh - 1)
        def _():
            down.wait_recv()

        placed = []
        for side in range(2):
            for j in range(per_row):
                x_in = rx[step, side, :, j * 128 : j * 128 + 128]
                placed.append(place(x_in, sh_high, side * per_row + j))
        return (applied + scatter(placed, sh_low)) * inv_mass

    start = v_ref[...]
    mass = mass_ref[...]
    turn_s[...] = jnp.zeros(turn_s.shape, f32)

    def masks():
        pass

    def first_column():
        level = first_s[...]
        lane = lax.broadcasted_iota(jnp.int32, (modes, 128), 1)
        turn_s[0:modes, :] = jnp.where(
            lane == 0, jnp.sum(mass * level * level, axis=1, keepdims=True), 0.0
        )

    first_s[...] = (operate(start, 0, masks) - center * start) * inv_half
    first = first_s[...]
    second_s[...] = 2.0 * (operate(first, 1, first_column) - center * first_s[...]) * inv_half - v_ref[...]

    first_sum = turn_s[0:modes, 0:1]
    edge_tx[:, 0:nodes] = second_s[modes - edge_count :, :]
    edge_tx[:, nodes:] = jnp.broadcast_to(first_sum[modes - edge_count :], (edge_count, 128))
    edge_copy = pltpu.make_async_remote_copy(
        src_ref=edge_tx,
        dst_ref=edge_rx,
        send_sem=edge_send,
        recv_sem=edge_recv,
        device_id={"cuts": lax.rem(cut + 1, n_cuts)},
        device_id_type=MESH,
    )

    @pl.when(cut < n_cuts - 1)
    def _():
        edge_copy.start()

    second = second_s[...]
    second_sum = jnp.sum(mass * second * second, axis=1, keepdims=True)

    def columns(a, b):
        lane = lax.broadcasted_iota(jnp.int32, (a.shape[0], 128), 1)
        return jnp.where(lane == 0, a, jnp.where(lane == 1, b, 0.0))

    turn_s[0:modes, :] = columns(first_sum, second_sum)

    @pl.when(cut > 0)
    def _():
        edge_copy.wait_recv()

    received = edge_rx[:, 0:nodes]
    weighted = received * mass
    turn_s[modes : modes + edge_count, :] = columns(
        edge_rx[:, nodes:][:, 0:1], jnp.sum(weighted * received, axis=1, keepdims=True)
    )
    left = jnp.concatenate(split2(weighted), axis=0)
    right = jnp.concatenate(split2(second_s[0:edge_count, :]), axis=0)
    inner = lax.dot_general(
        left, right, (((1,), (1,)), ((), ())), preferred_element_type=f32
    )
    inner = inner[0:edge_count] + inner[edge_count:]
    inner = inner[:, 0:edge_count] + inner[:, edge_count:]
    turn_s[modes + edge_count : modes + 2 * edge_count, 0:edge_count] = inner
    block[...] = turn_s[...].T[0:8]

    def sum_copy(i, target):
        return pltpu.make_async_remote_copy(
            src_ref=block,
            dst_ref=blocks.at[me],
            send_sem=sum_send.at[i],
            recv_sem=sum_recv.at[me],
            device_id={"mesh": target},
            device_id_type=MESH,
        )

    def arrival(i):
        return pltpu.make_async_remote_copy(
            src_ref=block,
            dst_ref=blocks.at[i],
            send_sem=sum_send.at[i],
            recv_sem=sum_recv.at[i],
            device_id={"mesh": i},
            device_id_type=MESH,
        )

    def each(act):
        def step(i, carry):
            target = jnp.where(me < n_mesh // 2, n_mesh - 1 - i, i)

            @pl.when(target != me)
            def _():
                act(i, target)

            return carry

        lax.fori_loop(0, n_mesh, step, 0, unroll=8)

    each(lambda i, target: sum_copy(i, target).start())
    blocks[me] = block[...]
    each(lambda i, target: arrival(target).wait_recv())
    total = lax.fori_loop(1, n_mesh, lambda i, acc: acc + blocks[i], blocks[0])

    total_ref[...] = total

    for step in range(2):
        up, down = halo(step)

        @pl.when(me < n_mesh - 1)
        def _():
            up.wait_send()

        @pl.when(me > 0)
        def _():
            down.wait_send()

    @pl.when(cut < n_cuts - 1)
    def _():
        edge_copy.wait_send()

    each(lambda i, target: sum_copy(i, target).wait_send())


def finish(total_nodes, first_ref, second_ref, total_ref, keep_ref, filt_ref, edge_ref, level_ref):
    modes = first_ref.shape[0]
    edge_count = keep_ref.shape[1]
    total = jnp.concatenate([total_ref[...], jnp.zeros((120, 128), f32)], axis=0).T
    scale = lax.rsqrt(total[:, 0:1] / total_nodes + epsilon)
    own = scale * lax.rsqrt(scale * scale * total[:, 1:2] / total_nodes + epsilon)
    level_ref[...] = first_ref[...] * scale[0:modes]
    filt_ref[...] = second_ref[...] * own[0:modes]
    eye = lax.broadcasted_iota(jnp.int32, (modes, modes), 0) == lax.broadcasted_iota(
        jnp.int32, (modes, modes), 1
    )
    own_row = jnp.sum(
        jnp.where(eye, jnp.broadcast_to(own[0:modes], (modes, modes)), 0.0),
        axis=0,
        keepdims=True,
    )
    products = (
        total[modes + edge_count : modes + 2 * edge_count, 0:edge_count]
        * own[modes : modes + edge_count]
        * own_row[:, 0:edge_count]
        * keep_ref[...].astype(f32)
        * (1.0 / math.sqrt(total_nodes))
    )
    edge_ref[0] = products


def per_device(
    start_modes,
    connectivity,
    stiffness_weights,
    shared_nodes,
    node_mass,
    centers,
    half_widths,
    keep_flags,
):
    n_mesh = lax.axis_size("mesh")
    n_cuts = lax.axis_size("cuts")
    modes, nodes = start_modes.shape
    local, elements = connectivity.shape
    shared = shared_nodes.shape[1]
    edge_count = keep_flags.shape[1]
    padded = -(-local // 8) * 8
    chunks = padded * elements // 128
    pairs = 2 * shared // 128
    vmem = pl.BlockSpec(memory_space=pltpu.VMEM)
    dma = pltpu.SemaphoreType.DMA
    first, second, total = pl.pallas_call(
        functools.partial(kernel, n_mesh, n_cuts, nodes * n_mesh),
        out_shape=(
            pltpu.VMEM((modes, nodes), f32),
            pltpu.VMEM((modes, nodes), f32),
            pltpu.VMEM((8, 128), f32),
        ),
        in_specs=[vmem] * 7,
        out_specs=(vmem, vmem, vmem),
        scratch_shapes=[
            pltpu.VMEM((128, 128), f32),
            pltpu.VMEM((padded, elements), jnp.int32),
            pltpu.VMEM((chunks, 128), f32),
            pltpu.VMEM((chunks, 128), f32),
            pltpu.VMEM((pairs, 128), f32),
            pltpu.VMEM((pairs, 128), f32),
            pltpu.VMEM((padded, 8, 128), f32),
            pltpu.VMEM((padded, 8, 128), f32),
            pltpu.VMEM((padded, 8, 128), f32),
            pltpu.VMEM((2, 2, modes, shared), f32),
            pltpu.VMEM((2, 2, modes, shared), f32),
            pltpu.VMEM((edge_count, nodes + 128), f32),
            pltpu.VMEM((edge_count, nodes + 128), f32),
            pltpu.VMEM((8, 128), f32),
            pltpu.VMEM((n_mesh, 8, 128), f32),
            dma((2, 2)),
            dma((2, 2)),
            dma,
            dma,
            dma((n_mesh,)),
            dma((n_mesh,)),
        ],
        compiler_params=pltpu.CompilerParams(collective_id=0, has_side_effects=True),
    )(
        start_modes,
        connectivity.T,
        stiffness_weights.T,
        shared_nodes,
        node_mass.reshape(1, nodes),
        centers.reshape(1, 1),
        half_widths.reshape(1, 1),
    )
    first, second, total = (
        pltpu.with_memory_space_constraint(x, pltpu.VMEM) for x in (first, second, total)
    )
    return pl.pallas_call(
        functools.partial(finish, nodes * n_mesh),
        out_shape=(
            jax.ShapeDtypeStruct((modes, nodes), f32),
            jax.ShapeDtypeStruct((1, edge_count, edge_count), f32),
            jax.ShapeDtypeStruct((modes, nodes), f32),
        ),
        in_specs=[vmem, vmem, vmem, vmem],
        out_specs=(vmem, vmem, vmem),
    )(first, second, total, keep_flags)


def solution(mesh):
    return jax.shard_map(
        per_device,
        mesh=mesh,
        in_specs=(
            P("cuts", "mesh"),
            P(None, "mesh"),
            P(None, "mesh"),
            P(None, "mesh"),
            P("mesh"),
            P("cuts"),
            P("cuts"),
            P("cuts", None),
        ),
        out_specs=(P("cuts", "mesh"), P("cuts", None, None), P("cuts", "mesh")),
        check_vma=False,
    )
```

```python
import functools
import math

import jax
import jax.numpy as jnp
import numpy as np
from jax import lax
from jax.experimental import pallas as pl
from jax.experimental.pallas import tpu as pltpu
from jax.sharding import PartitionSpec as P

epsilon = 1e-06
TILE = 256
MESH = pl.DeviceIdType.MESH
bf16 = jnp.bfloat16
f32 = jnp.float32


def gll_derivative():
    points = np.array([-1.0, -math.sqrt(3.0 / 7.0), 0.0, math.sqrt(3.0 / 7.0), 1.0])
    barycentric = np.array(
        [1.0 / np.prod([points[j] - points[k] for k in range(5) if k != j]) for j in range(5)]
    )
    table = np.zeros((5, 5))
    for row_index in range(5):
        for col_index in range(5):
            if row_index != col_index:
                table[row_index, col_index] = (
                    barycentric[col_index]
                    / barycentric[row_index]
                    / (points[row_index] - points[col_index])
                )
        table[row_index, row_index] = -np.sum(table[row_index])
    return table


def apply5(table, u):
    even = [u[0] + u[4], u[1] + u[3]]
    odd = [u[0] - u[4], u[1] - u[3]]
    out = [None] * 5
    for i in range(2):
        s = [float((table[i, j] + table[i, 4 - j]) / 2) for j in range(2)]
        t = [float((table[i, j] - table[i, 4 - j]) / 2) for j in range(2)]
        p = s[0] * even[0] + s[1] * even[1] + float(table[i, 2]) * u[2]
        q = t[0] * odd[0] + t[1] * odd[1]
        out[i] = q + p
        out[4 - i] = q - p
    t = [float((table[2, j] - table[2, 4 - j]) / 2) for j in range(2)]
    out[2] = t[0] * odd[0] + t[1] * odd[1]
    return out


def transpose4(x):
    block = lax.broadcasted_iota(jnp.int32, x[0].shape, 1) // 32
    at = [block == b for b in range(3)]
    y = [x[0]] + [pltpu.roll(x[g], 32 * g, 1) for g in range(1, 4)]
    z = []
    for q in range(4):
        w = y[(3 - q) % 4]
        for b in range(3):
            w = jnp.where(at[b], y[(b - q) % 4], w)
        z.append(w if q == 0 else pltpu.roll(w, 128 - 32 * q, 1))
    return z


def split2(x):
    high = x.astype(bf16)
    low = (x - high.astype(f32)).astype(bf16)
    return high, low


def kernel(
    n_mesh,
    n_cuts,
    total_nodes,
    v_ref,
    conn_ref,
    w_ref,
    shared_ref,
    mass_ref,
    center_ref,
    half_ref,
    first_s,
    second_s,
    total_ref,
    turn_s,
    conn_s,
    low_s,
    high_s,
    sh_low,
    sh_high,
    w_s,
    u_s,
    r_s,
    tx,
    rx,
    edge_tx,
    edge_rx,
    block,
    blocks,
    halo_send,
    halo_recv,
    edge_send,
    edge_recv,
    sum_send,
    sum_recv,
):
    me = lax.axis_index("mesh")
    cut = lax.axis_index("cuts")
    modes, nodes = v_ref.shape
    groups = modes // 8
    low_size = 2 * TILE if nodes % (2 * TILE) == 0 else TILE
    highs = nodes // low_size
    shift = low_size.bit_length() - 1
    elements, local = conn_ref.shape
    shared = shared_ref.shape[1]
    edge_count = edge_tx.shape[0]
    table = gll_derivative()

    barrier = pltpu.get_barrier_semaphore()

    def greet(d, carry):
        pl.semaphore_signal(
            barrier,
            inc=1,
            device_id={"mesh": lax.rem(me + d, n_mesh)},
            device_id_type=MESH,
        )
        return carry

    lax.fori_loop(1, n_mesh, greet, 0)

    @pl.when(cut > 0)
    def _():
        pl.semaphore_signal(
            barrier, inc=1, device_id={"cuts": cut - 1}, device_id_type=MESH
        )

    @pl.when(cut < n_cuts - 1)
    def _():
        pl.semaphore_signal(
            barrier, inc=1, device_id={"cuts": cut + 1}, device_id_type=MESH
        )

    turn_s[...] = jnp.full(turn_s.shape, -1.0, f32)
    turn_s[0:elements, 0:local] = conn_ref[...].astype(f32)
    turn_s[elements : 2 * elements, 0:local] = w_ref[...]
    turned = turn_s[...].T
    conn_s[...] = turned[:, 0:elements].astype(jnp.int32)
    chunks = conn_s.shape[0] // 4
    index = jnp.concatenate(
        [conn_s[pl.ds(q, chunks, stride=4), :] for q in range(4)], axis=1
    )
    iota = lax.broadcasted_iota(jnp.int32, (16, 128), 0)
    steps = [(iota + 16 * i).astype(f32).astype(bf16) for i in range(TILE // 16)]
    one = jnp.ones((16, 128), bf16)
    zero = jnp.zeros((16, 128), bf16)

    def onehot(low_ref, r):
        row = low_ref[r : r + 1, :]
        parts = []
        for t in range(low_size // TILE):
            wide = jnp.broadcast_to(row - float(TILE * t), (16, 128)).astype(bf16)
            parts += [jnp.where(step == wide, one, zero) for step in steps]
        return jnp.concatenate(parts, axis=0)

    low_s[...] = (index & (low_size - 1)).astype(f32)
    high_s[...] = (index >> shift).astype(f32)
    per_row = shared // 128
    for r in range(2 * per_row):
        side, at = r // per_row, r % per_row * 128
        row = shared_ref[side : side + 1, at : at + 128]
        sh_low[r : r + 1, :] = (row & (low_size - 1)).astype(f32)
        sh_high[r : r + 1, :] = (row >> shift).astype(f32)
    w4 = jnp.concatenate([turned[:, elements : 2 * elements]] * 4, axis=1)
    for k in range(local):
        w_s[k] = jnp.broadcast_to(w4[k : k + 1], (8, 128))
    r_s[local:] = jnp.zeros((r_s.shape[0] - local, 8, 128), f32)

    inv_mass = 1.0 / mass_ref[...]
    center = center_ref[...]
    inv_half = 1.0 / half_ref[...]

    rows = highs * modes

    def load_source(x):
        parts = split2(x)
        return jnp.concatenate(
            [y[:, h * low_size : (h + 1) * low_size] for y in parts for h in range(highs)], axis=0
        )

    def gather(left, low_ref, high_ref, t):
        right = jnp.concatenate([onehot(low_ref, 2 * t), onehot(low_ref, 2 * t + 1)], axis=1)
        res = jnp.dot(left, right, preferred_element_type=f32)
        res = res[0:rows] + res[rows:]
        out = []
        for half in range(2):
            at = 2 * t + half
            high = jnp.broadcast_to(high_ref[at : at + 1, :], (8, 128))
            cols = slice(half * 128, half * 128 + 128)
            sides = [high == h for h in range(1, highs)]
            groups_out = []
            for g in range(groups):
                pick = res[g * 8 : g * 8 + 8, cols]
                for h in range(1, highs):
                    at = h * modes + g * 8
                    pick = jnp.where(sides[h - 1], res[at : at + 8, cols], pick)
                groups_out.append(pick)
            out.append(groups_out)
        return out

    def place(x, high_ref, r):
        high = jnp.broadcast_to(high_ref[r : r + 1, :], (16, 128)).astype(bf16)
        parts = split2(x)
        out = []
        for h in range(highs):
            here = high == jnp.full((16, 128), h, bf16)
            for y in parts:
                for i in range(modes // 16):
                    out.append(jnp.where(here, y[i * 16 : i * 16 + 16], zero))
        return jnp.concatenate(out, axis=0)

    def scatter(placed, low_ref):
        res = lax.dot_general(
            jnp.concatenate(placed, axis=1),
            jnp.concatenate([onehot(low_ref, r) for r in range(len(placed))], axis=1),
            (((1,), (1,)), ((), ())),
            preferred_element_type=f32,
        )
        return jnp.concatenate(
            [
                res[h * 2 * modes : h * 2 * modes + modes]
                + res[h * 2 * modes + modes : (h + 1) * 2 * modes]
                for h in range(highs)
            ],
            axis=1,
        )

    def line(u, w):
        g = apply5(table, u)
        return apply5(table.T, [g[i] * w[i] for i in range(5)])

    def element_pass():
        for a in range(5):
            u = [u_s[25 * a + j] for j in range(25)]
            w = [w_s[25 * a + j] for j in range(25)]
            r = [None] * 25
            for b in range(5):
                r[5 * b : 5 * b + 5] = line(u[5 * b : 5 * b + 5], w[5 * b : 5 * b + 5])
            for c in range(5):
                back = line(u[c::5], w[c::5])
                for b in range(5):
                    r_s[25 * a + 5 * b + c] = r[5 * b + c] + back[b]
        for j in range(25):
            back = line([u_s[25 * a + j] for a in range(5)], [w_s[25 * a + j] for a in range(5)])
            for a in range(5):
                r_s[25 * a + j] = r_s[25 * a + j] + back[a]

    def halo(step):
        up = pltpu.make_async_remote_copy(
            src_ref=tx.at[step, 1],
            dst_ref=rx.at[step, 0],
            send_sem=halo_send.at[step, 0],
            recv_sem=halo_recv.at[step, 0],
            device_id={"mesh": lax.rem(me + 1, n_mesh)},
            device_id_type=MESH,
        )
        down = pltpu.make_async_remote_copy(
            src_ref=tx.at[step, 0],
            dst_ref=rx.at[step, 1],
            send_sem=halo_send.at[step, 1],
            recv_sem=halo_recv.at[step, 1],
            device_id={"mesh": lax.rem(me + n_mesh - 1, n_mesh)},
            device_id_type=MESH,
        )
        return up, down

    @pl.when(me == 0)
    def _():
        for step in range(2):
            rx[step, 0] = jnp.zeros((modes, shared), f32)

    @pl.when(me == n_mesh - 1)
    def _():
        for step in range(2):
            rx[step, 1] = jnp.zeros((modes, shared), f32)

    @pl.when(cut == 0)
    def _():
        edge_rx[...] = jnp.zeros(edge_rx.shape, f32)

    def operate(x, step, between):
        left = load_source(x)
        for t in range(chunks // 2):
            out = gather(left, low_s, high_s, t)
            for half in range(2):
                r = 2 * t + half
                for q, y in enumerate(transpose4(out[half])):
                    u_s[4 * r + q] = y
        element_pass()
        placed = []
        for r in range(chunks):
            piece = transpose4([r_s[4 * r + q] for q in range(4)])
            placed.append(place(jnp.concatenate(piece, axis=0), high_s, r))
        applied = scatter(placed, low_s)
        left = load_source(applied)
        up, down = halo(step)
        for t in range(2 * shared // 256):
            out = gather(left, sh_low, sh_high, t)
            at = t * 256
            tx[step, at // shared, :, at % shared : at % shared + 256] = jnp.concatenate(
                [jnp.concatenate(half, axis=0) for half in out], axis=1
            )
            if at + 256 == shared:
                if step == 0:
                    pl.semaphore_wait(
                        barrier,
                        n_mesh - 1 + jnp.minimum(cut, 1) + jnp.minimum(n_cuts - 1 - cut, 1),
                    )

                @pl.when(me > 0)
                def _():
                    down.start()

        @pl.when(me < n_mesh - 1)
        def _():
            up.start()

        between()

        @pl.when(me > 0)
        def _():
            up.wait_recv()

        @pl.when(me < n_mesh - 1)
        def _():
            down.wait_recv()

        placed = []
        for side in range(2):
            for j in range(per_row):
                x_in = rx[step, side, :, j * 128 : j * 128 + 128]
                placed.append(place(x_in, sh_high, side * per_row + j))
        return (applied + scatter(placed, sh_low)) * inv_mass

    start = v_ref[...]
    mass = mass_ref[...]
    turn_s[...] = jnp.zeros(turn_s.shape, f32)

    def masks():
        pass

    def first_column():
        level = first_s[...]
        turn_s[0:modes, :] = jnp.broadcast_to(
            jnp.sum(mass * level * level, axis=1, keepdims=True), (modes, 128)
        )

    first_s[...] = (operate(start, 0, masks) - center * start) * inv_half
    first = first_s[...]
    second_s[...] = 2.0 * (operate(first, 1, first_column) - center * first_s[...]) * inv_half - v_ref[...]

    first_sum = turn_s[0:modes, 0:1]
    edge_tx[:, 0:nodes] = second_s[modes - edge_count :, :]
    edge_tx[:, nodes:] = jnp.broadcast_to(first_sum[modes - edge_count :], (edge_count, 128))
    edge_copy = pltpu.make_async_remote_copy(
        src_ref=edge_tx,
        dst_ref=edge_rx,
        send_sem=edge_send,
        recv_sem=edge_recv,
        device_id={"cuts": lax.rem(cut + 1, n_cuts)},
        device_id_type=MESH,
    )

    @pl.when(cut < n_cuts - 1)
    def _():
        edge_copy.start()

    second = second_s[...]
    second_sum = jnp.sum(mass * second * second, axis=1, keepdims=True)

    below = slice(modes, modes + edge_count)
    at_second = edge_count + groups
    at_edge = edge_count + 2 * groups

    @pl.when(cut > 0)
    def _():
        edge_copy.wait_recv()
        received = edge_rx[:, 0:nodes]
        weighted = received * mass
        turn_s[below, at_edge : at_edge + 1] = edge_rx[:, nodes : nodes + 1]
        turn_s[below, at_edge + 1 : at_edge + 2] = jnp.sum(
            weighted * received, axis=1, keepdims=True
        )
        left = jnp.concatenate(split2(weighted), axis=0)
        right = jnp.concatenate(split2(second_s[0:edge_count, :]), axis=0)
        inner = lax.dot_general(
            left, right, (((1,), (1,)), ((), ())), preferred_element_type=f32
        )
        inner = inner[0:edge_count] + inner[edge_count:]
        turn_s[below, 0:edge_count] = inner[:, 0:edge_count] + inner[:, edge_count:]

    lane = lax.broadcasted_iota(jnp.int32, (8, 128), 1)
    packed = turn_s[below, :]
    for g in range(groups):
        of = slice(g * 8, g * 8 + 8)
        packed = jnp.where(lane == edge_count + g, turn_s[of, :], packed)
        packed = jnp.where(lane == at_second + g, second_sum[of], packed)
    block[...] = packed

    def sum_copy(i, target):
        return pltpu.make_async_remote_copy(
            src_ref=block,
            dst_ref=blocks.at[me],
            send_sem=sum_send.at[i],
            recv_sem=sum_recv.at[me],
            device_id={"mesh": target},
            device_id_type=MESH,
        )

    def arrival(i):
        return pltpu.make_async_remote_copy(
            src_ref=block,
            dst_ref=blocks.at[i],
            send_sem=sum_send.at[i],
            recv_sem=sum_recv.at[i],
            device_id={"mesh": i},
            device_id_type=MESH,
        )

    def each(act):
        def step(i, carry):
            target = jnp.where(me < n_mesh // 2, n_mesh - 1 - i, i)

            @pl.when(target != me)
            def _():
                act(i, target)

            return carry

        lax.fori_loop(0, n_mesh, step, 0, unroll=8)

    each(lambda i, target: sum_copy(i, target).start())
    blocks[me] = block[...]
    each(lambda i, target: arrival(target).wait_recv())
    total = lax.fori_loop(1, n_mesh, lambda i, acc: acc + blocks[i], blocks[0])

    total_ref[...] = total

    for step in range(2):
        up, down = halo(step)

        @pl.when(me < n_mesh - 1)
        def _():
            up.wait_send()

        @pl.when(me > 0)
        def _():
            down.wait_send()

    @pl.when(cut < n_cuts - 1)
    def _():
        edge_copy.wait_send()

    each(lambda i, target: sum_copy(i, target).wait_send())


def finish(total_nodes, first_ref, second_ref, total_ref, keep_ref, filt_ref, edge_ref, level_ref):
    modes = first_ref.shape[0]
    edge_count = keep_ref.shape[1]
    groups = modes // 8

    def factors(at_first, at_second):
        first_sum = total_ref[:, at_first : at_first + 1]
        second_sum = total_ref[:, at_second : at_second + 1]
        scale = lax.rsqrt(first_sum / total_nodes + epsilon)
        return scale, scale * lax.rsqrt(scale * scale * second_sum / total_nodes + epsilon)

    lower = None
    for g in range(groups):
        of = slice(g * 8, g * 8 + 8)
        scale, own = factors(edge_count + g, edge_count + groups + g)
        level_ref[of, :] = first_ref[of, :] * scale
        filt_ref[of, :] = second_ref[of, :] * own
        lower = own if g == 0 else lower
    _, upper = factors(edge_count + 2 * groups, edge_count + 2 * groups + 1)
    square = (edge_count, edge_count)
    eye = lax.broadcasted_iota(jnp.int32, square, 0) == lax.broadcasted_iota(
        jnp.int32, square, 1
    )
    lower_row = jnp.sum(
        jnp.where(eye, jnp.broadcast_to(lower, square), 0.0), axis=0, keepdims=True
    )
    edge_ref[0] = (
        total_ref[:, 0:edge_count]
        * upper
        * lower_row
        * keep_ref[...].astype(f32)
        * (1.0 / math.sqrt(total_nodes))
    )


def per_device(
    start_modes,
    connectivity,
    stiffness_weights,
    shared_nodes,
    node_mass,
    centers,
    half_widths,
    keep_flags,
):
    n_mesh = lax.axis_size("mesh")
    n_cuts = lax.axis_size("cuts")
    modes, nodes = start_modes.shape
    local, elements = connectivity.shape
    shared = shared_nodes.shape[1]
    edge_count = keep_flags.shape[1]
    padded = -(-local // 8) * 8
    chunks = padded * elements // 128
    pairs = 2 * shared // 128
    vmem = pl.BlockSpec(memory_space=pltpu.VMEM)
    dma = pltpu.SemaphoreType.DMA
    first, second, total = pl.pallas_call(
        functools.partial(kernel, n_mesh, n_cuts, nodes * n_mesh),
        out_shape=(
            pltpu.VMEM((modes, nodes), f32),
            pltpu.VMEM((modes, nodes), f32),
            pltpu.VMEM((8, 128), f32),
        ),
        in_specs=[vmem] * 7,
        out_specs=(vmem, vmem, vmem),
        scratch_shapes=[
            pltpu.VMEM((128, 128), f32),
            pltpu.VMEM((padded, elements), jnp.int32),
            pltpu.VMEM((chunks, 128), f32),
            pltpu.VMEM((chunks, 128), f32),
            pltpu.VMEM((pairs, 128), f32),
            pltpu.VMEM((pairs, 128), f32),
            pltpu.VMEM((padded, 8, 128), f32),
            pltpu.VMEM((padded, 8, 128), f32),
            pltpu.VMEM((padded, 8, 128), f32),
            pltpu.VMEM((2, 2, modes, shared), f32),
            pltpu.VMEM((2, 2, modes, shared), f32),
            pltpu.VMEM((edge_count, nodes + 128), f32),
            pltpu.VMEM((edge_count, nodes + 128), f32),
            pltpu.VMEM((8, 128), f32),
            pltpu.VMEM((n_mesh, 8, 128), f32),
            dma((2, 2)),
            dma((2, 2)),
            dma,
            dma,
            dma((n_mesh,)),
            dma((n_mesh,)),
        ],
        compiler_params=pltpu.CompilerParams(collective_id=0, has_side_effects=True),
    )(
        start_modes,
        connectivity.T,
        stiffness_weights.T,
        shared_nodes,
        node_mass.reshape(1, nodes),
        centers.reshape(1, 1),
        half_widths.reshape(1, 1),
    )
    first, second, total = (
        pltpu.with_memory_space_constraint(x, pltpu.VMEM) for x in (first, second, total)
    )
    return pl.pallas_call(
        functools.partial(finish, nodes * n_mesh),
        out_shape=(
            jax.ShapeDtypeStruct((modes, nodes), f32),
            jax.ShapeDtypeStruct((1, edge_count, edge_count), f32),
            jax.ShapeDtypeStruct((modes, nodes), f32),
        ),
        in_specs=[vmem, vmem, vmem, vmem],
        out_specs=(vmem, vmem, vmem),
    )(first, second, total, keep_flags)


def solution(mesh):
    return jax.shard_map(
        per_device,
        mesh=mesh,
        in_specs=(
            P("cuts", "mesh"),
            P(None, "mesh"),
            P(None, "mesh"),
            P(None, "mesh"),
            P("mesh"),
            P("cuts"),
            P("cuts"),
            P("cuts", None),
        ),
        out_specs=(P("cuts", "mesh"), P("cuts", None, None), P("cuts", "mesh")),
        check_vma=False,
    )
```

```python
import functools
import math

import jax
import jax.numpy as jnp
import numpy as np
from jax import lax
from jax.experimental import pallas as pl
from jax.experimental.pallas import tpu as pltpu
from jax.sharding import PartitionSpec as P

epsilon = 1e-06
TILE = 256
MESH = pl.DeviceIdType.MESH
bf16 = jnp.bfloat16
f32 = jnp.float32


def gll_derivative():
    points = np.array([-1.0, -math.sqrt(3.0 / 7.0), 0.0, math.sqrt(3.0 / 7.0), 1.0])
    barycentric = np.array(
        [1.0 / np.prod([points[j] - points[k] for k in range(5) if k != j]) for j in range(5)]
    )
    table = np.zeros((5, 5))
    for row_index in range(5):
        for col_index in range(5):
            if row_index != col_index:
                table[row_index, col_index] = (
                    barycentric[col_index]
                    / barycentric[row_index]
                    / (points[row_index] - points[col_index])
                )
        table[row_index, row_index] = -np.sum(table[row_index])
    return table


def halves_of(table):
    s = [[(table[i, j] + table[i, 4 - j]) / 2 for j in range(2)] for i in range(2)]
    t = [[(table[i, j] - table[i, 4 - j]) / 2 for j in range(2)] for i in range(3)]
    return s, t, [s[0][0], s[1][1], t[2][1]]


def apply5(table, u, w):
    s, t, unit = halves_of(table)
    s01, s10, t20 = float(s[0][1] / unit[0]), float(s[1][0] / unit[1]), float(t[2][0] / unit[2])
    tt = [[float(t[i][j] / unit[i]) for j in range(2)] for i in range(2)]
    twice = u[2] + u[2]
    e0, e1 = u[0] + u[4] - twice, u[1] + u[3] - twice
    o0, o1 = u[0] - u[4], u[1] - u[3]
    p0, p1 = e0 + s01 * e1, e1 + s10 * e0
    q0, q1 = tt[0][0] * o0 + tt[0][1] * o1, tt[1][0] * o0 + tt[1][1] * o1
    g = [q0 + p0, q1 + p1, t20 * o0 + o1, q1 - p1, q0 - p0]
    g = [g[i] * w[i] for i in range(5)]
    p0, p1 = g[0] - g[4], g[1] - g[3]
    q0, q1 = g[0] + g[4], g[1] + g[3]
    a0, a1 = p0 + s10 * p1, p1 + s01 * p0
    b0 = tt[0][0] * q0 + tt[1][0] * q1 + t20 * g[2]
    b1 = tt[0][1] * q0 + tt[1][1] * q1 + g[2]
    return [a0 + b0, a1 + b1, -2.0 * (a0 + a1), a1 - b1, a0 - b0]


def transpose4(x):
    block = lax.broadcasted_iota(jnp.int32, x[0].shape, 1) // 32
    at = [block == b for b in range(3)]
    y = [x[0]] + [pltpu.roll(x[g], 32 * g, 1) for g in range(1, 4)]
    z = []
    for q in range(4):
        w = y[(3 - q) % 4]
        for b in range(3):
            w = jnp.where(at[b], y[(b - q) % 4], w)
        z.append(w if q == 0 else pltpu.roll(w, 128 - 32 * q, 1))
    return z


def split2(x):
    high = x.astype(bf16)
    low = (x - high.astype(f32)).astype(bf16)
    return high, low


def kernel(
    n_mesh,
    n_cuts,
    total_nodes,
    v_ref,
    conn_ref,
    w_ref,
    shared_ref,
    mass_ref,
    center_ref,
    half_ref,
    first_s,
    second_s,
    total_ref,
    turn_s,
    conn_s,
    low_s,
    high_s,
    sh_low,
    sh_high,
    w_s,
    u_s,
    r_s,
    tx,
    rx,
    edge_tx,
    edge_rx,
    block,
    blocks,
    halo_send,
    halo_recv,
    edge_send,
    edge_recv,
    sum_send,
    sum_recv,
):
    me = lax.axis_index("mesh")
    cut = lax.axis_index("cuts")
    modes, nodes = v_ref.shape
    groups = modes // 8
    low_size = 2 * TILE if nodes % (2 * TILE) == 0 else TILE
    highs = nodes // low_size
    shift = low_size.bit_length() - 1
    elements, local = conn_ref.shape
    shared = shared_ref.shape[1]
    edge_count = edge_tx.shape[0]
    table = gll_derivative()

    barrier = pltpu.get_barrier_semaphore()

    def greet(d, carry):
        pl.semaphore_signal(
            barrier,
            inc=1,
            device_id={"mesh": lax.rem(me + d, n_mesh)},
            device_id_type=MESH,
        )
        return carry

    lax.fori_loop(1, n_mesh, greet, 0)

    @pl.when(cut > 0)
    def _():
        pl.semaphore_signal(
            barrier, inc=1, device_id={"cuts": cut - 1}, device_id_type=MESH
        )

    @pl.when(cut < n_cuts - 1)
    def _():
        pl.semaphore_signal(
            barrier, inc=1, device_id={"cuts": cut + 1}, device_id_type=MESH
        )

    turn_s[...] = jnp.full(turn_s.shape, -1.0, f32)
    turn_s[0:elements, 0:local] = conn_ref[...].astype(f32)
    turn_s[elements : 2 * elements, 0:local] = w_ref[...]
    turned = turn_s[...].T
    conn_s[...] = turned[:, 0:elements].astype(jnp.int32)
    chunks = conn_s.shape[0] // 4
    index = jnp.concatenate(
        [conn_s[pl.ds(q, chunks, stride=4), :] for q in range(4)], axis=1
    )
    iota = lax.broadcasted_iota(jnp.int32, (16, 128), 0)
    steps = [(iota + 16 * i).astype(f32).astype(bf16) for i in range(TILE // 16)]
    one = jnp.ones((16, 128), bf16)
    zero = jnp.zeros((16, 128), bf16)

    def onehot(low_ref, r):
        row = low_ref[r : r + 1, :]
        parts = []
        for t in range(low_size // TILE):
            wide = jnp.broadcast_to(row - float(TILE * t), (16, 128)).astype(bf16)
            parts += [jnp.where(step == wide, one, zero) for step in steps]
        return jnp.concatenate(parts, axis=0)

    low_s[...] = (index & (low_size - 1)).astype(f32)
    high_s[...] = (index >> shift).astype(f32)
    per_row = shared // 128
    for r in range(2 * per_row):
        side, at = r // per_row, r % per_row * 128
        row = shared_ref[side : side + 1, at : at + 128]
        sh_low[r : r + 1, :] = (row & (low_size - 1)).astype(f32)
        sh_high[r : r + 1, :] = (row >> shift).astype(f32)
    w4 = jnp.concatenate([turned[:, elements : 2 * elements]] * 4, axis=1)
    for k in range(local):
        base = jnp.broadcast_to(w4[k : k + 1], (8, 128))
        for axis, i in enumerate((k // 25, k // 5 % 5, k % 5)):
            w_s[axis, k] = base * float(halves_of(table)[2][min(i, 4 - i)] ** 2)
    r_s[local:] = jnp.zeros((r_s.shape[0] - local, 8, 128), f32)

    inv_mass = 1.0 / mass_ref[...]
    center = center_ref[...]
    inv_half = 1.0 / half_ref[...]

    rows = highs * modes

    def load_source(x):
        parts = split2(x)
        return jnp.concatenate(
            [y[:, h * low_size : (h + 1) * low_size] for y in parts for h in range(highs)], axis=0
        )

    def gather(left, low_ref, high_ref, t):
        right = jnp.concatenate([onehot(low_ref, 2 * t), onehot(low_ref, 2 * t + 1)], axis=1)
        res = jnp.dot(left, right, preferred_element_type=f32)
        res = res[0:rows] + res[rows:]
        out = []
        for half in range(2):
            at = 2 * t + half
            high = jnp.broadcast_to(high_ref[at : at + 1, :], (8, 128))
            cols = slice(half * 128, half * 128 + 128)
            sides = [high == h for h in range(1, highs)]
            groups_out = []
            for g in range(groups):
                pick = res[g * 8 : g * 8 + 8, cols]
                for h in range(1, highs):
                    at = h * modes + g * 8
                    pick = jnp.where(sides[h - 1], res[at : at + 8, cols], pick)
                groups_out.append(pick)
            out.append(groups_out)
        return out

    def place(x, high_ref, r):
        high = jnp.broadcast_to(high_ref[r : r + 1, :], (16, 128)).astype(bf16)
        parts = split2(x)
        out = []
        for h in range(highs):
            here = high == jnp.full((16, 128), h, bf16)
            for y in parts:
                for i in range(modes // 16):
                    out.append(jnp.where(here, y[i * 16 : i * 16 + 16], zero))
        return jnp.concatenate(out, axis=0)

    def scatter(placed, low_ref):
        res = lax.dot_general(
            jnp.concatenate(placed, axis=1),
            jnp.concatenate([onehot(low_ref, r) for r in range(len(placed))], axis=1),
            (((1,), (1,)), ((), ())),
            preferred_element_type=f32,
        )
        return jnp.concatenate(
            [
                res[h * 2 * modes : h * 2 * modes + modes]
                + res[h * 2 * modes + modes : (h + 1) * 2 * modes]
                for h in range(highs)
            ],
            axis=1,
        )

    line = functools.partial(apply5, table)

    def element_pass():
        for a in range(5):
            u = [u_s[25 * a + j] for j in range(25)]
            w = [[w_s[axis, 25 * a + j] for j in range(25)] for axis in (1, 2)]
            r = [None] * 25
            for b in range(5):
                r[5 * b : 5 * b + 5] = line(u[5 * b : 5 * b + 5], w[1][5 * b : 5 * b + 5])
            for c in range(5):
                back = line(u[c::5], w[0][c::5])
                for b in range(5):
                    r_s[25 * a + 5 * b + c] = r[5 * b + c] + back[b]
        for j in range(25):
            back = line([u_s[25 * a + j] for a in range(5)], [w_s[0, 25 * a + j] for a in range(5)])
            for a in range(5):
                r_s[25 * a + j] = r_s[25 * a + j] + back[a]

    def halo(step):
        up = pltpu.make_async_remote_copy(
            src_ref=tx.at[step, 1],
            dst_ref=rx.at[step, 0],
            send_sem=halo_send.at[step, 0],
            recv_sem=halo_recv.at[step, 0],
            device_id={"mesh": lax.rem(me + 1, n_mesh)},
            device_id_type=MESH,
        )
        down = pltpu.make_async_remote_copy(
            src_ref=tx.at[step, 0],
            dst_ref=rx.at[step, 1],
            send_sem=halo_send.at[step, 1],
            recv_sem=halo_recv.at[step, 1],
            device_id={"mesh": lax.rem(me + n_mesh - 1, n_mesh)},
            device_id_type=MESH,
        )
        return up, down

    @pl.when(me == 0)
    def _():
        for step in range(2):
            rx[step, 0] = jnp.zeros((modes, shared), f32)

    @pl.when(me == n_mesh - 1)
    def _():
        for step in range(2):
            rx[step, 1] = jnp.zeros((modes, shared), f32)

    @pl.when(cut == 0)
    def _():
        edge_rx[...] = jnp.zeros(edge_rx.shape, f32)

    def operate(x, step, between):
        left = load_source(x)
        for t in range(chunks // 2):
            out = gather(left, low_s, high_s, t)
            for half in range(2):
                r = 2 * t + half
                for q, y in enumerate(transpose4(out[half])):
                    u_s[4 * r + q] = y
        element_pass()
        placed = []
        for r in range(chunks):
            piece = transpose4([r_s[4 * r + q] for q in range(4)])
            placed.append(place(jnp.concatenate(piece, axis=0), high_s, r))
        applied = scatter(placed, low_s)
        left = load_source(applied)
        up, down = halo(step)
        for t in range(2 * shared // 256):
            out = gather(left, sh_low, sh_high, t)
            at = t * 256
            tx[step, at // shared, :, at % shared : at % shared + 256] = jnp.concatenate(
                [jnp.concatenate(half, axis=0) for half in out], axis=1
            )
            if at + 256 == shared:
                if step == 0:
                    pl.semaphore_wait(
                        barrier,
                        n_mesh - 1 + jnp.minimum(cut, 1) + jnp.minimum(n_cuts - 1 - cut, 1),
                    )

                @pl.when(me > 0)
                def _():
                    down.start()

        @pl.when(me < n_mesh - 1)
        def _():
            up.start()

        between()

        @pl.when(me > 0)
        def _():
            up.wait_recv()

        @pl.when(me < n_mesh - 1)
        def _():
            down.wait_recv()

        placed = []
        for side in range(2):
            for j in range(per_row):
                x_in = rx[step, side, :, j * 128 : j * 128 + 128]
                placed.append(place(x_in, sh_high, side * per_row + j))
        return (applied + scatter(placed, sh_low)) * inv_mass

    start = v_ref[...]
    mass = mass_ref[...]
    turn_s[...] = jnp.zeros(turn_s.shape, f32)

    def masks():
        pass

    def first_column():
        level = first_s[...]
        turn_s[0:modes, :] = jnp.broadcast_to(
            jnp.sum(mass * level * level, axis=1, keepdims=True), (modes, 128)
        )

    first_s[...] = (operate(start, 0, masks) - center * start) * inv_half
    first = first_s[...]
    second_s[...] = 2.0 * (operate(first, 1, first_column) - center * first_s[...]) * inv_half - v_ref[...]

    first_sum = turn_s[0:modes, 0:1]
    edge_tx[:, 0:nodes] = second_s[modes - edge_count :, :]
    edge_tx[:, nodes:] = jnp.broadcast_to(first_sum[modes - edge_count :], (edge_count, 128))
    edge_copy = pltpu.make_async_remote_copy(
        src_ref=edge_tx,
        dst_ref=edge_rx,
        send_sem=edge_send,
        recv_sem=edge_recv,
        device_id={"cuts": lax.rem(cut + 1, n_cuts)},
        device_id_type=MESH,
    )

    @pl.when(cut < n_cuts - 1)
    def _():
        edge_copy.start()

    second = second_s[...]
    second_sum = jnp.sum(mass * second * second, axis=1, keepdims=True)

    below = slice(modes, modes + edge_count)
    at_second = edge_count + groups
    at_edge = edge_count + 2 * groups

    @pl.when(cut > 0)
    def _():
        edge_copy.wait_recv()
        received = edge_rx[:, 0:nodes]
        weighted = received * mass
        turn_s[below, at_edge : at_edge + 1] = edge_rx[:, nodes : nodes + 1]
        turn_s[below, at_edge + 1 : at_edge + 2] = jnp.sum(
            weighted * received, axis=1, keepdims=True
        )
        left = jnp.concatenate(split2(weighted), axis=0)
        right = jnp.concatenate(split2(second_s[0:edge_count, :]), axis=0)
        inner = lax.dot_general(
            left, right, (((1,), (1,)), ((), ())), preferred_element_type=f32
        )
        inner = inner[0:edge_count] + inner[edge_count:]
        turn_s[below, 0:edge_count] = inner[:, 0:edge_count] + inner[:, edge_count:]

    lane = lax.broadcasted_iota(jnp.int32, (8, 128), 1)
    packed = turn_s[below, :]
    for g in range(groups):
        of = slice(g * 8, g * 8 + 8)
        packed = jnp.where(lane == edge_count + g, turn_s[of, :], packed)
        packed = jnp.where(lane == at_second + g, second_sum[of], packed)
    block[...] = packed

    def sum_copy(i, target):
        return pltpu.make_async_remote_copy(
            src_ref=block,
            dst_ref=blocks.at[me],
            send_sem=sum_send.at[i],
            recv_sem=sum_recv.at[me],
            device_id={"mesh": target},
            device_id_type=MESH,
        )

    def arrival(i):
        return pltpu.make_async_remote_copy(
            src_ref=block,
            dst_ref=blocks.at[i],
            send_sem=sum_send.at[i],
            recv_sem=sum_recv.at[i],
            device_id={"mesh": i},
            device_id_type=MESH,
        )

    def each(act):
        def step(i, carry):
            target = jnp.where(me < n_mesh // 2, n_mesh - 1 - i, i)

            @pl.when(target != me)
            def _():
                act(i, target)

            return carry

        lax.fori_loop(0, n_mesh, step, 0, unroll=8)

    each(lambda i, target: sum_copy(i, target).start())
    blocks[me] = block[...]
    each(lambda i, target: arrival(target).wait_recv())
    total = lax.fori_loop(1, n_mesh, lambda i, acc: acc + blocks[i], blocks[0])

    total_ref[...] = total

    for step in range(2):
        up, down = halo(step)

        @pl.when(me < n_mesh - 1)
        def _():
            up.wait_send()

        @pl.when(me > 0)
        def _():
            down.wait_send()

    @pl.when(cut < n_cuts - 1)
    def _():
        edge_copy.wait_send()

    each(lambda i, target: sum_copy(i, target).wait_send())


def finish(total_nodes, first_ref, second_ref, total_ref, keep_ref, filt_ref, edge_ref, level_ref):
    modes = first_ref.shape[0]
    edge_count = keep_ref.shape[1]
    groups = modes // 8

    def factors(at_first, at_second):
        first_sum = total_ref[:, at_first : at_first + 1]
        second_sum = total_ref[:, at_second : at_second + 1]
        scale = lax.rsqrt(first_sum / total_nodes + epsilon)
        return scale, scale * lax.rsqrt(scale * scale * second_sum / total_nodes + epsilon)

    lower = None
    for g in range(groups):
        of = slice(g * 8, g * 8 + 8)
        scale, own = factors(edge_count + g, edge_count + groups + g)
        level_ref[of, :] = first_ref[of, :] * scale
        filt_ref[of, :] = second_ref[of, :] * own
        lower = own if g == 0 else lower
    _, upper = factors(edge_count + 2 * groups, edge_count + 2 * groups + 1)
    square = (edge_count, edge_count)
    eye = lax.broadcasted_iota(jnp.int32, square, 0) == lax.broadcasted_iota(
        jnp.int32, square, 1
    )
    lower_row = jnp.sum(
        jnp.where(eye, jnp.broadcast_to(lower, square), 0.0), axis=0, keepdims=True
    )
    edge_ref[0] = (
        total_ref[:, 0:edge_count]
        * upper
        * lower_row
        * keep_ref[...].astype(f32)
        * (1.0 / math.sqrt(total_nodes))
    )


def per_device(
    start_modes,
    connectivity,
    stiffness_weights,
    shared_nodes,
    node_mass,
    centers,
    half_widths,
    keep_flags,
):
    n_mesh = lax.axis_size("mesh")
    n_cuts = lax.axis_size("cuts")
    modes, nodes = start_modes.shape
    local, elements = connectivity.shape
    shared = shared_nodes.shape[1]
    edge_count = keep_flags.shape[1]
    padded = -(-local // 8) * 8
    chunks = padded * elements // 128
    pairs = 2 * shared // 128
    vmem = pl.BlockSpec(memory_space=pltpu.VMEM)
    dma = pltpu.SemaphoreType.DMA
    first, second, total = pl.pallas_call(
        functools.partial(kernel, n_mesh, n_cuts, nodes * n_mesh),
        out_shape=(
            pltpu.VMEM((modes, nodes), f32),
            pltpu.VMEM((modes, nodes), f32),
            pltpu.VMEM((8, 128), f32),
        ),
        in_specs=[vmem] * 7,
        out_specs=(vmem, vmem, vmem),
        scratch_shapes=[
            pltpu.VMEM((128, 128), f32),
            pltpu.VMEM((padded, elements), jnp.int32),
            pltpu.VMEM((chunks, 128), f32),
            pltpu.VMEM((chunks, 128), f32),
            pltpu.VMEM((pairs, 128), f32),
            pltpu.VMEM((pairs, 128), f32),
            pltpu.VMEM((3, padded, 8, 128), f32),
            pltpu.VMEM((padded, 8, 128), f32),
            pltpu.VMEM((padded, 8, 128), f32),
            pltpu.VMEM((2, 2, modes, shared), f32),
            pltpu.VMEM((2, 2, modes, shared), f32),
            pltpu.VMEM((edge_count, nodes + 128), f32),
            pltpu.VMEM((edge_count, nodes + 128), f32),
            pltpu.VMEM((8, 128), f32),
            pltpu.VMEM((n_mesh, 8, 128), f32),
            dma((2, 2)),
            dma((2, 2)),
            dma,
            dma,
            dma((n_mesh,)),
            dma((n_mesh,)),
        ],
        compiler_params=pltpu.CompilerParams(collective_id=0, has_side_effects=True),
    )(
        start_modes,
        connectivity.T,
        stiffness_weights.T,
        shared_nodes,
        node_mass.reshape(1, nodes),
        centers.reshape(1, 1),
        half_widths.reshape(1, 1),
    )
    first, second, total = (
        pltpu.with_memory_space_constraint(x, pltpu.VMEM) for x in (first, second, total)
    )
    return pl.pallas_call(
        functools.partial(finish, nodes * n_mesh),
        out_shape=(
            jax.ShapeDtypeStruct((modes, nodes), f32),
            jax.ShapeDtypeStruct((1, edge_count, edge_count), f32),
            jax.ShapeDtypeStruct((modes, nodes), f32),
        ),
        in_specs=[vmem, vmem, vmem, vmem],
        out_specs=(vmem, vmem, vmem),
    )(first, second, total, keep_flags)


def solution(mesh):
    return jax.shard_map(
        per_device,
        mesh=mesh,
        in_specs=(
            P("cuts", "mesh"),
            P(None, "mesh"),
            P(None, "mesh"),
            P(None, "mesh"),
            P("mesh"),
            P("cuts"),
            P("cuts"),
            P("cuts", None),
        ),
        out_specs=(P("cuts", "mesh"), P("cuts", None, None), P("cuts", "mesh")),
        check_vma=False,
    )
```
